32 devices in a mesh: gx: 4 (over x, core), gy: 8 (over z, y).
Axes of the slice: x: 2, y: 2, z: 4, core: 2. Of those that a mesh axis runs over, the one named last changes fastest.
Arguments:
- tokens: bfloat16 [2740, 1024], P('gx', 'gy'), may hold values from -64 to 64
- cotangent: bfloat16 [2740, 1024], P('gx', 'gy'), may hold values from -6 to 6
- norm1_gain: float32 [1024], P('gy'), may hold values from 0.1 to 1.9
- norm1_shift: float32 [1024], P('gy'), may hold values from -1.5 to 1.5
- qkv_weight: bfloat16 [1024, 3072], P('gx', 'gy'), may hold values from -4 to 4
- qv_bias: float32 [2048], P('gy'), may hold values from -2.5 to 2.5
- proj_weight: bfloat16 [1024, 1024], P('gx', 'gy'), may hold values from -1.5 to 1.5
- proj_bias: float32 [1024], P('gy'), may hold values from -1.5 to 1.5
- scale_attn: float32 [1024], P('gy'), may hold values from 0.3 to 1.5
- norm2_gain: float32 [1024], P('gy'), may hold values from 0.1 to 1.9
- norm2_shift: float32 [1024], P('gy'), may hold values from -1.5 to 1.5
- fc1_weight: bfloat16 [1024, 4096], P('gx', 'gy'), may hold values from -0.1875 to 0.1875
- fc1_bias: float32 [4096], P('gy'), may hold values from -2.5 to 2.5
- fc2_weight: bfloat16 [4096, 1024], P('gx', 'gy'), may hold values from -0.09375 to 0.09375
- fc2_bias: float32 [1024], P('gy'), may hold values from -1.5 to 1.5
- scale_mlp: float32 [1024], P('gy'), may hold values from 0.3 to 1.5
Outputs:
- output: float32 [2740, 1024], P('gx', 'gy')
- grad_tokens: float32 [2740, 1024], P('gx', 'gy')
- grad_norm1_gain: float32 [1024], P('gy')
- grad_norm1_shift: float32 [1024], P('gy')
- grad_qkv_weight: float32 [1024, 3072], P('gx', 'gy')
- grad_qv_bias: float32 [2048], P('gy')
- grad_proj_weight: float32 [1024, 1024], P('gx', 'gy')
- grad_proj_bias: float32 [1024], P('gy')
- grad_scale_attn: float32 [1024], P('gy')
- grad_norm2_gain: float32 [1024], P('gy')
- grad_norm2_shift: float32 [1024], P('gy')
- grad_fc1_weight: float32 [1024, 4096], P('gx', 'gy')
- grad_fc1_bias: float32 [4096], P('gy')
- grad_fc2_weight: float32 [4096, 1024], P('gx', 'gy')
- grad_fc2_bias: float32 [1024], P('gy')
- grad_scale_mlp: float32 [1024], P('gy')
The draws below stay inside these ranges and needn't reach their ends.
All inputs are finite; a program needn't handle non-finite values.
Results may differ from the reference program's by a relative error of at most 0.012.
Values may be sent and summed in bfloat16 or wider, within the bound.
A program may use at most 128 MiB of HBM per device.

```python
import math
import jax
import jax.numpy as jnp
from jax import lax

D = 1024
HEADS = 16
HD = 64
FF = 4096
SEQ = 1370
IMGS = 1
TOKENS = 2740


def draw_tokens(key, part):
    subkeys = jax.random.split(key, 3)
    lowest = math.log(0.4)
    highest = math.log(4.0)
    row_scale = jnp.exp(jax.random.uniform(subkeys[0], (TOKENS, 1), jnp.float32, lowest, highest))
    col_scale = jnp.exp(jax.random.uniform(subkeys[1], (1, D), jnp.float32, lowest, highest))
    sample = jnp.clip(jax.random.normal(subkeys[2], (TOKENS, D), jnp.float32), -4.0, 4.0)
    return (sample * row_scale * col_scale).astype(jnp.bfloat16)


def draw_qkv_weight(key, part):
    subkeys = jax.random.split(key, 1)
    sample = jnp.clip(jax.random.normal(subkeys[0], (D, HEADS, 3, HD), jnp.float32), -4.0, 4.0) * D ** (-0.5)
    return jnp.clip(sample, -4.0, 4.0).reshape(D, 3 * D).astype(jnp.bfloat16)


def shard_levels(own_key, extent, pieces, smallest, high):
    loudness, own = 1.0, jax.random.fold_in(own_key, 6)
    for axis_at, shards_of in pieces:
        steps = jnp.exp(jax.random.uniform(jax.random.fold_in(own, axis_at), (shards_of,), jnp.float32, smallest / len(pieces), high / len(pieces)))
        loudness = loudness * jnp.repeat(steps, extent[axis_at] // shards_of).reshape([-1 if axis == axis_at else 1 for axis in range(len(extent))])
    return loudness


def centred(key, dims, width, most, cuts=(), kind=jnp.bfloat16):
    drawn = width * jax.random.normal(key, dims, jnp.float32)
    if cuts:
        drawn = drawn * shard_levels(key, dims, cuts, -0.22, 0.18)
    return jnp.clip(drawn, -most, most).astype(kind)


def setup_inputs(seed: int = 0) -> dict:
    splits = jax.random.split(jax.random.key(seed), 17)
    tokens = draw_tokens(jax.random.fold_in(splits[16], 71), 0)
    cotangent = centred(splits[1], (TOKENS, D), 1.0, 6.0, ((0, 4), (1, 8)))
    norm1_gain = jnp.clip(1.0 + 0.18 * jax.random.normal(splits[2], (D,), jnp.float32), 0.1, 1.9)
    norm1_shift = centred(splits[3], (D,), 0.3, 1.5, ((0, 8),), jnp.float32)
    qkv_weight = draw_qkv_weight(jax.random.fold_in(splits[16], 71), 0)
    qv_bias = centred(splits[5], (2 * D,), 0.5, 2.5, ((0, 8),), jnp.float32)
    proj_weight = centred(splits[6], (D, D), (HD // 4) ** -0.5, 1.5, ((0, 4), (1, 8)))
    proj_bias = centred(splits[7], (D,), 0.3, 1.5, ((0, 8),), jnp.float32)
    scale_attn = jnp.clip(jnp.exp(math.log(1.5) - 1.60943787 * jax.random.uniform(splits[8], (D,), jnp.float32) ** shard_levels(splits[8], (D,), ((0, 8),), -0.2, 0.2)), 0.3, 1.5)
    norm2_gain = jnp.clip(1.0 + 0.18 * jax.random.normal(splits[9], (D,), jnp.float32), 0.1, 1.9)
    norm2_shift = centred(splits[10], (D,), 0.3, 1.5, ((0, 8),), jnp.float32)
    fc1_weight = centred(splits[11], (D, FF), D ** -0.5, 0.1875, ((0, 4), (1, 8)))
    fc1_bias = centred(splits[12], (FF,), 0.5, 2.5, ((0, 8),), jnp.float32)
    fc2_weight = centred(splits[13], (FF, D), FF ** -0.5, 0.09375, ((0, 4), (1, 8)))
    fc2_bias = centred(splits[14], (D,), 0.3, 1.5, ((0, 8),), jnp.float32)
    scale_mlp = jnp.clip(jnp.exp(math.log(1.5) - 1.60943787 * jax.random.uniform(splits[15], (D,), jnp.float32) ** shard_levels(splits[15], (D,), ((0, 8),), -0.2, 0.2)), 0.3, 1.5)
    return dict(tokens=tokens, cotangent=cotangent, norm1_gain=norm1_gain, norm1_shift=norm1_shift, qkv_weight=qkv_weight, qv_bias=qv_bias, proj_weight=proj_weight, proj_bias=proj_bias, scale_attn=scale_attn, norm2_gain=norm2_gain, norm2_shift=norm2_shift, fc1_weight=fc1_weight, fc1_bias=fc1_bias, fc2_weight=fc2_weight, fc2_bias=fc2_bias, scale_mlp=scale_mlp)


EPS = 1e-06
ROOT_HALF = 0.7071067811865476
INV_ROOT_TAU = 0.3989422804014327

def normal_cdf(values):
    return 0.5 * (1.0 + jax.scipy.special.erf(values * ROOT_HALF))

def gelu_exact(values):
    return values * normal_cdf(values)

def gelu_slope(values):
    return normal_cdf(values) + values * jnp.exp(-0.5 * values * values) * INV_ROOT_TAU

def round_keep(values):
    return lax.optimization_barrier(values.astype(jnp.bfloat16)).astype(jnp.float32)

def to_images(array):
    half_len = SEQ // 2
    groups = array.shape[0] // (2 * IMGS * half_len)
    shaped = array.reshape(groups, 2, IMGS, half_len, array.shape[1])
    return jnp.transpose(shaped, (0, 2, 1, 3, 4)).reshape(array.shape[0], array.shape[1])

def from_images(array):
    half_len = SEQ // 2
    groups = array.shape[0] // (2 * IMGS * half_len)
    shaped = array.reshape(groups, IMGS, 2, half_len, array.shape[1])
    return jnp.transpose(shaped, (0, 2, 1, 3, 4)).reshape(array.shape[0], array.shape[1])

def norm_forward(rows, gain, shift):
    row_mean = lax.optimization_barrier(jnp.mean(rows, axis=1, keepdims=True))
    centered = rows - row_mean
    inv_std = lax.rsqrt(lax.optimization_barrier(jnp.mean(centered * centered, axis=1, keepdims=True)) + EPS)
    normed = centered * inv_std
    return (normed, inv_std, (normed * gain + shift).astype(jnp.bfloat16))

def norm_backward(grad_normed, normed, inv_std, gain):
    scaled = grad_normed * gain
    first = lax.optimization_barrier(jnp.mean(scaled, axis=1, keepdims=True))
    second = lax.optimization_barrier(jnp.mean(scaled * normed, axis=1, keepdims=True))
    return inv_std * (scaled - first - normed * second)

def attend(blocks):
    queries, keys, values = blocks
    scores = jnp.einsum('qhe,khe->hqk', queries.astype(jnp.float32), keys.astype(jnp.float32)) * HD ** (-0.5)
    row_max = lax.optimization_barrier(jnp.max(scores, axis=2, keepdims=True))
    exponent = jnp.exp(scores - row_max)
    totals = lax.optimization_barrier(jnp.sum(exponent, axis=2, keepdims=True))
    probs = round_keep(exponent / totals)
    attended = jnp.einsum('hqk,khe->qhe', probs, values.astype(jnp.float32)).astype(jnp.bfloat16)
    return (attended, row_max + jnp.log(totals))

def attend_back(blocks):
    queries, keys, values, attended, log_total, grad_att = blocks
    scores = jnp.einsum('qhe,khe->hqk', queries.astype(jnp.float32), keys.astype(jnp.float32)) * HD ** (-0.5)
    recomputed = jnp.exp(scores - log_total)
    probs_b = round_keep(recomputed)
    grad_att_f = grad_att.astype(jnp.float32)
    grad_values = jnp.einsum('hqk,qhe->khe', probs_b, grad_att_f)
    grad_probs = jnp.einsum('qhe,khe->hqk', grad_att_f, values.astype(jnp.float32))
    delta = lax.optimization_barrier(jnp.sum(grad_att_f * attended.astype(jnp.float32), axis=2))
    grad_scores = recomputed * (grad_probs - jnp.transpose(delta)[:, :, None])
    grad_scores_b = round_keep(grad_scores)
    grad_queries = jnp.einsum('hqk,khe->qhe', grad_scores_b, keys.astype(jnp.float32)) * HD ** (-0.5)
    grad_keys = jnp.einsum('hqk,qhe->khe', grad_scores_b, queries.astype(jnp.float32)) * HD ** (-0.5)
    return (grad_queries, grad_keys, grad_values)

def reference(tokens, cotangent, norm1_gain, norm1_shift, qkv_weight, qv_bias, proj_weight, proj_bias, scale_attn, norm2_gain, norm2_shift, fc1_weight, fc1_bias, fc2_weight, fc2_bias, scale_mlp):
    count = tokens.shape[0]
    images = count // SEQ
    inputs = to_images(tokens).astype(jnp.float32)
    upstream = to_images(cotangent).astype(jnp.float32)
    normed_one, inv_one, norm_one = norm_forward(inputs, norm1_gain, norm1_shift)
    mixed = jnp.dot(norm_one, qkv_weight, preferred_element_type=jnp.float32).reshape(count, HEADS, 3, HD)
    biases = qv_bias.reshape(HEADS, 2, HD)
    queries = (mixed[:, :, 0] + biases[:, 0]).astype(jnp.bfloat16).reshape(images, SEQ, HEADS, HD)
    keys = mixed[:, :, 1].astype(jnp.bfloat16).reshape(images, SEQ, HEADS, HD)
    values = (mixed[:, :, 2] + biases[:, 1]).astype(jnp.bfloat16).reshape(images, SEQ, HEADS, HD)
    attended, log_total = lax.map(attend, (queries, keys, values))
    attended_flat = attended.reshape(count, D)
    attn_out = jnp.dot(attended_flat, proj_weight, preferred_element_type=jnp.float32) + proj_bias
    middle = inputs + scale_attn * attn_out
    normed_two, inv_two, norm_two = norm_forward(middle, norm2_gain, norm2_shift)
    pre_act = jnp.dot(norm_two, fc1_weight, preferred_element_type=jnp.float32) + fc1_bias
    hidden = gelu_exact(pre_act).astype(jnp.bfloat16)
    mlp_out = jnp.dot(hidden, fc2_weight, preferred_element_type=jnp.float32) + fc2_bias
    output = middle + scale_mlp * mlp_out
    grad_scale_mlp = lax.optimization_barrier(jnp.sum(upstream * mlp_out, axis=0))
    grad_mlp = upstream * scale_mlp
    grad_fc2_bias = lax.optimization_barrier(jnp.sum(grad_mlp, axis=0))
    grad_mlp_b = grad_mlp.astype(jnp.bfloat16)
    grad_fc2 = jnp.dot(hidden.T, grad_mlp_b, preferred_element_type=jnp.float32)
    grad_hidden = jnp.dot(grad_mlp_b, fc2_weight.T, preferred_element_type=jnp.float32)
    grad_pre = grad_hidden * gelu_slope(pre_act)
    grad_fc1_bias = lax.optimization_barrier(jnp.sum(grad_pre, axis=0))
    grad_pre_b = grad_pre.astype(jnp.bfloat16)
    grad_fc1 = jnp.dot(norm_two.T, grad_pre_b, preferred_element_type=jnp.float32)
    grad_norm_two = jnp.dot(grad_pre_b, fc1_weight.T, preferred_element_type=jnp.float32)
    grad_gain_two = lax.optimization_barrier(jnp.sum(grad_norm_two * normed_two, axis=0))
    grad_shift_two = lax.optimization_barrier(jnp.sum(grad_norm_two, axis=0))
    grad_middle = upstream + norm_backward(grad_norm_two, normed_two, inv_two, norm2_gain)
    grad_scale_attn = lax.optimization_barrier(jnp.sum(grad_middle * attn_out, axis=0))
    grad_attn = grad_middle * scale_attn
    grad_proj_bias = lax.optimization_barrier(jnp.sum(grad_attn, axis=0))
    grad_attn_b = grad_attn.astype(jnp.bfloat16)
    grad_proj = jnp.dot(attended_flat.T, grad_attn_b, preferred_element_type=jnp.float32)
    grad_attended = jnp.dot(grad_attn_b, proj_weight.T, preferred_element_type=jnp.float32).astype(jnp.bfloat16)
    grad_queries, grad_keys, grad_values = lax.map(attend_back, (queries, keys, values, attended, log_total, grad_attended.reshape(images, SEQ, HEADS, HD)))
    grad_queries = grad_queries.reshape(count, HEADS, HD)
    grad_keys = grad_keys.reshape(count, HEADS, HD)
    grad_values = grad_values.reshape(count, HEADS, HD)
    grad_qv_bias = jnp.stack([lax.optimization_barrier(jnp.sum(grad_queries, axis=0)), lax.optimization_barrier(jnp.sum(grad_values, axis=0))], axis=1).reshape(2 * D)
    grad_mixed = jnp.stack([grad_queries, grad_keys, grad_values], axis=2).astype(jnp.bfloat16).reshape(count, 3 * D)
    grad_qkv = jnp.dot(norm_one.T, grad_mixed, preferred_element_type=jnp.float32)
    grad_norm_one = jnp.dot(grad_mixed, qkv_weight.T, preferred_element_type=jnp.float32)
    grad_gain_one = lax.optimization_barrier(jnp.sum(grad_norm_one * normed_one, axis=0))
    grad_shift_one = lax.optimization_barrier(jnp.sum(grad_norm_one, axis=0))
    grad_input = grad_middle + norm_backward(grad_norm_one, normed_one, inv_one, norm1_gain)
    return (from_images(output), from_images(grad_input), grad_gain_one, grad_shift_one, grad_qkv, grad_qv_bias, grad_proj, grad_proj_bias, grad_scale_attn, grad_gain_two, grad_shift_two, grad_fc1, grad_fc1_bias, grad_fc2, grad_fc2_bias, grad_scale_mlp)
```

```python
import functools

import jax
import jax.numpy as jnp
from jax import lax
from jax.experimental import pallas as pl
from jax.experimental.pallas import tpu as pltpu
from jax.sharding import PartitionSpec as P

D = 1024
HD = 64
IMGS = 1


EPS = 1e-06
ROOT_HALF = 0.7071067811865476
INV_ROOT_TAU = 0.3989422804014327


def from_partner(block, axis, bit):
    count = lax.axis_size(axis)
    route = []
    for low in range(count):
        high = low | 1 << bit
        if high != low and high < count:
            route += [(low, high), (high, low)]
    return lax.ppermute(block, axis, route)


def normal_cdf(values):
    return 0.5 * (1.0 + jax.scipy.special.erf(values * ROOT_HALF))


def gelu_exact(values):
    return values * normal_cdf(values)


def gelu_slope(values):
    return normal_cdf(values) + values * jnp.exp(-0.5 * values * values) * INV_ROOT_TAU


def norm_full(rows, gain, shift):
    row_mean = jnp.mean(rows, axis=1, keepdims=True)
    inv_std = lax.rsqrt(jnp.mean(rows * rows, axis=1, keepdims=True) - row_mean * row_mean + EPS)
    normed = (rows - row_mean) * inv_std
    return (normed, inv_std, (normed * gain + shift).astype(jnp.bfloat16))


def gather_columns(block):
    return lax.all_gather(block, "gy", axis=1, tiled=True)


def ring_kernel(parts, block_ref, out_ref, send_sem, recv_sem):
    half = parts // 2

    def index_of(place):
        back = place // half
        return (1 - back) * (2 * place) + back * (2 * (parts - 1 - place) + 1)

    me = lax.axis_index("gy")
    odd = me % 2
    place = (1 - odd) * (me // 2) + odd * (parts - 1 - me // 2)
    sides = (index_of((place + 1) % parts), index_of((place + parts - 1) % parts))
    barrier = pltpu.get_barrier_semaphore()
    for side in sides:
        pl.semaphore_signal(
            barrier, inc=1, device_id={"gy": side}, device_id_type=pl.DeviceIdType.MESH
        )
    pl.semaphore_wait(barrier, 2)
    copies = []
    for step in range(half):
        owners = (
            index_of((place + parts - step) % parts),
            index_of((place + step) % parts),
        )
        started = []
        for way in range(2):
            if way == 1 and step == half - 1:
                continue
            copy = pltpu.make_async_remote_copy(
                src_ref=block_ref if step == 0 else out_ref.at[owners[way]],
                dst_ref=out_ref.at[owners[way]],
                send_sem=send_sem.at[way, step],
                recv_sem=recv_sem.at[way, step],
                device_id={"gy": sides[way]},
                device_id_type=pl.DeviceIdType.MESH,
            )
            copy.start()
            started.append(copy)
        if step == 0:
            out_ref[me] = block_ref[...]
        for copy in started:
            copy.wait_recv()
        copies += started
    for copy in copies:
        copy.wait_send()


def ring_columns(block, call):
    parts = lax.axis_size("gy")
    count, width = block.shape
    if parts % 2 or parts < 4:
        return gather_columns(block)
    got = pl.pallas_call(
        functools.partial(ring_kernel, parts),
        out_shape=jax.ShapeDtypeStruct((parts, count, width), block.dtype),
        in_specs=[pl.BlockSpec(memory_space=pltpu.VMEM)],
        out_specs=pl.BlockSpec(memory_space=pltpu.VMEM),
        scratch_shapes=[
            pltpu.SemaphoreType.DMA((2, parts // 2)),
            pltpu.SemaphoreType.DMA((2, parts // 2)),
        ],
        compiler_params=pltpu.CompilerParams(collective_id=call, has_side_effects=True),
    )(block)
    return jnp.transpose(got, (1, 0, 2)).reshape(count, parts * width)


def spread_columns(block):
    parts = lax.axis_size("gy")
    got = lax.all_to_all(
        jnp.broadcast_to(block[None], (parts,) + block.shape), "gy", 0, 0, tiled=True
    )
    return jnp.transpose(got, (1, 0, 2)).reshape(block.shape[0], parts * block.shape[1])


def column_blocks(block):
    parts = lax.axis_size("gy")
    count, full = block.shape
    return jnp.transpose(block.reshape(count, parts, full // parts), (1, 0, 2))


def scatter_sum(blocks, axis):
    got = lax.all_to_all(blocks, axis, 0, 0, tiled=True)
    return jnp.sum(got.astype(jnp.float32), axis=0)


def own_columns(block, width):
    return lax.dynamic_slice_in_dim(block, lax.axis_index("gy") * width, width, axis=1)


def sum_rows(term):
    parts = lax.axis_size("gx")
    blocks = term.reshape(parts, term.shape[0] // parts, term.shape[1])
    return scatter_sum(blocks, "gx")


def weight_grad_rows(saved, grad_out):
    term = jnp.einsum("tk,tn->kn", saved, grad_out, preferred_element_type=jnp.float32)
    return lax.psum_scatter(
        term.astype(jnp.bfloat16), "gx", scatter_dimension=0, tiled=True
    ).astype(jnp.float32)


def weight_grad(saved, grad_out):
    term = jnp.einsum("tk,tn->kn", saved, grad_out, preferred_element_type=jnp.float32)
    return sum_rows(term.astype(jnp.bfloat16))


def lanes_of(column, width):
    count = column.shape[0]
    lines = -(-count // width)
    return jnp.pad(column, (0, lines * width - count)).reshape(lines, width)


def back_norm(grad_out, weight, normed, normed_own, inv_std, gain, gain_own):
    parts = lax.axis_size("gy")
    count, full = normed.shape
    width = full // parts
    term = jnp.einsum("tn,kn->tk", grad_out, weight, preferred_element_type=jnp.float32)
    scaled = term * gain
    first = lanes_of(jnp.sum(scaled, axis=1), width)
    second = lanes_of(jnp.sum(scaled * normed, axis=1), width)
    lines = first.shape[0]
    sums = jnp.concatenate([first, second], axis=0).astype(jnp.bfloat16)
    blocks = column_blocks(term.astype(jnp.bfloat16))
    sent = jnp.concatenate(
        [blocks, jnp.broadcast_to(sums[None], (parts,) + sums.shape)], axis=1
    )
    back = scatter_sum(sent, "gy")
    grad_normed = back[:count]
    first = back[count : count + lines].reshape(-1)[:count, None]
    second = back[count + lines :].reshape(-1)[:count, None]
    grad_rows = inv_std * (
        grad_normed * gain_own - first / full - normed_own * (second / full)
    )
    return (
        grad_rows,
        jnp.sum(grad_normed * normed_own, axis=0),
        jnp.sum(grad_normed, axis=0),
    )


def on_device(
    tokens,
    cotangent,
    norm1_gain,
    norm1_shift,
    qkv_weight,
    qv_bias,
    proj_weight,
    proj_bias,
    scale_attn,
    norm2_gain,
    norm2_shift,
    fc1_weight,
    fc1_bias,
    fc2_weight,
    fc2_bias,
    scale_mlp,
):
    count = tokens.shape[0]
    half_len = count // IMGS
    heads_here = qkv_weight.shape[1] // (3 * HD)
    factor = HD ** (-0.5)
    width = tokens.shape[1]
    full_tokens = ring_columns(tokens, 0)
    vectors = spread_columns(
        jnp.stack([norm1_gain, norm1_shift, proj_bias, scale_attn, norm2_gain, norm2_shift, scale_mlp])
    )
    gain_one, shift_one, bias_proj, full_scale_attn, gain_two, shift_two, full_scale_mlp = vectors
    full_qkv = lax.all_gather(qkv_weight, "gx", axis=0, tiled=True)
    all_proj = lax.all_gather(ring_columns(proj_weight, 1), "gx", axis=0, tiled=True)
    full_fc1 = lax.all_gather(fc1_weight, "gx", axis=0, tiled=True)
    full_fc2 = lax.all_gather(fc2_weight, "gx", axis=0, tiled=True)
    rows_fc2 = lax.all_to_all(full_fc2, "gy", split_axis=0, concat_axis=1, tiled=True)
    full_cotangent = gather_columns(cotangent)
    inputs = full_tokens.astype(jnp.float32)
    normed_one, inv_one, norm_one = norm_full(inputs, gain_one, shift_one)
    mixed = jnp.dot(norm_one, full_qkv, preferred_element_type=jnp.float32)
    mixed = mixed.reshape(count, heads_here, 3, HD)
    biases = qv_bias.reshape(heads_here, 2, HD)
    queries = (mixed[:, :, 0] + biases[:, 0]).astype(jnp.bfloat16)
    keys = mixed[:, :, 1].astype(jnp.bfloat16)
    values = (mixed[:, :, 2] + biases[:, 1]).astype(jnp.bfloat16)
    lower = lax.axis_index("gx") % 2 == 0
    pair_kv = jnp.concatenate([keys, values], axis=2).reshape(count, heads_here * 2 * HD)
    other_kv = from_partner(pair_kv, "gx", 0)
    first_kv = jnp.where(lower, pair_kv, other_kv)
    second_kv = jnp.where(lower, other_kv, pair_kv)
    image_shape = (IMGS, half_len, heads_here, 2 * HD)
    both_kv = jnp.concatenate(
        [first_kv.reshape(image_shape), second_kv.reshape(image_shape)], axis=1
    )
    key_all = both_kv[..., :HD]
    value_all = both_kv[..., HD:]
    query_img = queries.reshape(IMGS, half_len, heads_here, HD)
    scores = (
        jnp.einsum("iqhe,ikhe->ihqk", query_img, key_all, preferred_element_type=jnp.float32)
        * factor
    )
    row_max = jnp.max(scores, axis=3, keepdims=True)
    exponent = jnp.exp(scores - row_max)
    totals = jnp.sum(exponent, axis=3, keepdims=True)
    log_total = row_max + jnp.log(totals)
    probs = (exponent / totals).astype(jnp.bfloat16)
    attended_img = jnp.einsum(
        "ihqk,ikhe->iqhe", probs, value_all, preferred_element_type=jnp.float32
    ).astype(jnp.bfloat16)
    attended = attended_img.reshape(count, heads_here * HD)
    full_attended = ring_columns(attended, 0)
    attn_out = jnp.dot(full_attended, all_proj, preferred_element_type=jnp.float32) + bias_proj
    middle = inputs + full_scale_attn * attn_out
    normed_two, inv_two, norm_two = norm_full(middle, gain_two, shift_two)
    pre_act = jnp.dot(norm_two, full_fc1, preferred_element_type=jnp.float32) + fc1_bias
    hidden = gelu_exact(pre_act).astype(jnp.bfloat16)
    upstream = cotangent.astype(jnp.float32)
    grad_mlp = upstream * scale_mlp
    grad_fc2_bias = jnp.sum(grad_mlp, axis=0)
    full_grad_mlp_b = (full_cotangent.astype(jnp.float32) * full_scale_mlp).astype(jnp.bfloat16)
    grad_hidden = jnp.einsum(
        "tn,kn->tk", full_grad_mlp_b, rows_fc2, preferred_element_type=jnp.float32
    )
    grad_pre = grad_hidden * gelu_slope(pre_act)
    grad_fc1_bias = jnp.sum(grad_pre, axis=0)
    grad_pre_b = grad_pre.astype(jnp.bfloat16)
    own_two = own_columns(normed_two, width)
    grad_rows, grad_gain_two, grad_shift_two = back_norm(
        grad_pre_b, full_fc1, normed_two, own_two, inv_two, gain_two, norm2_gain
    )
    grad_middle = upstream + grad_rows
    grad_scale_attn = jnp.sum(grad_middle * own_columns(attn_out, width), axis=0)
    grad_attn = grad_middle * scale_attn
    grad_proj_bias = jnp.sum(grad_attn, axis=0)
    grad_attn_b = grad_attn.astype(jnp.bfloat16)
    full_grad_attn_b = ring_columns(grad_attn_b, 0)
    own_rows_proj = lax.dynamic_slice_in_dim(
        all_proj, lax.axis_index("gy") * width, width, axis=0
    )
    grad_attended = jnp.einsum(
        "tn,kn->tk", full_grad_attn_b, own_rows_proj, preferred_element_type=jnp.float32
    ).astype(jnp.bfloat16)
    mlp_term = jnp.dot(hidden, rows_fc2, preferred_element_type=jnp.float32)
    mlp_out = (
        lax.psum_scatter(
            column_blocks(mlp_term.astype(jnp.bfloat16)), "gy", scatter_dimension=0, tiled=False
        ).astype(jnp.float32)
        + fc2_bias
    )
    output = own_columns(middle, width) + scale_mlp * mlp_out
    grad_scale_mlp = jnp.sum(upstream * mlp_out, axis=0)
    fc2_term = jnp.einsum(
        "tk,tn->kn", hidden, full_grad_mlp_b, preferred_element_type=jnp.float32
    )
    fc2_blocks = lax.all_to_all(column_blocks(fc2_term.astype(jnp.bfloat16)), "gy", 0, 0, tiled=True)
    grad_fc2 = sum_rows(fc2_blocks.reshape(-1, width))
    grad_fc1 = weight_grad_rows(norm_two, grad_pre_b)
    grad_proj = weight_grad_rows(full_attended, grad_attn_b)
    grad_att_img = grad_attended.reshape(IMGS, half_len, heads_here, HD)
    recomputed = jnp.exp(scores - log_total)
    probs_b = recomputed.astype(jnp.bfloat16)
    grad_value_all = jnp.einsum(
        "ihqk,iqhe->ikhe", probs_b, grad_att_img, preferred_element_type=jnp.float32
    )
    grad_probs = jnp.einsum(
        "iqhe,ikhe->ihqk", grad_att_img, value_all, preferred_element_type=jnp.float32
    )
    delta = jnp.sum(grad_att_img.astype(jnp.float32) * attended_img.astype(jnp.float32), axis=3)
    grad_scores = recomputed * (grad_probs - jnp.transpose(delta, (0, 2, 1))[..., None])
    grad_scores_b = grad_scores.astype(jnp.bfloat16)
    grad_query = (
        jnp.einsum("ihqk,ikhe->iqhe", grad_scores_b, key_all, preferred_element_type=jnp.float32)
        * factor
    )
    grad_key_all = (
        jnp.einsum("ihqk,iqhe->ikhe", grad_scores_b, query_img, preferred_element_type=jnp.float32)
        * factor
    )
    grad_kv_all = jnp.concatenate([grad_key_all, grad_value_all], axis=3)
    first_part = grad_kv_all[:, :half_len].reshape(count, heads_here * 2 * HD)
    second_part = grad_kv_all[:, half_len:].reshape(count, heads_here * 2 * HD)
    own_part = jnp.where(lower, first_part, second_part)
    sent_part = jnp.where(lower, second_part, first_part)
    grad_kv = own_part + from_partner(sent_part.astype(jnp.bfloat16), "gx", 0).astype(
        sent_part.dtype
    )
    grad_kv = grad_kv.reshape(count, heads_here, 2, HD)
    grad_query = grad_query.reshape(count, heads_here, HD)
    grad_qv_bias = jnp.stack(
        [jnp.sum(grad_query, axis=0), jnp.sum(grad_kv[:, :, 1], axis=0)], axis=1
    ).reshape(heads_here * 2 * HD)
    grad_mixed = (
        jnp.stack([grad_query, grad_kv[:, :, 0], grad_kv[:, :, 1]], axis=2)
        .astype(jnp.bfloat16)
        .reshape(count, heads_here * 3 * HD)
    )
    grad_qkv = weight_grad(norm_one, grad_mixed)
    own_one = own_columns(normed_one, width)
    grad_rows, grad_gain_one, grad_shift_one = back_norm(
        grad_mixed, full_qkv, normed_one, own_one, inv_one, gain_one, norm1_gain
    )
    grad_input = grad_middle + grad_rows
    smalls = lax.psum(
        (
            grad_gain_one,
            grad_shift_one,
            grad_qv_bias,
            grad_proj_bias,
            grad_scale_attn,
            grad_gain_two,
            grad_shift_two,
            grad_fc1_bias,
            grad_fc2_bias,
            grad_scale_mlp,
        ),
        "gx",
    )
    return (
        output,
        grad_input,
        smalls[0],
        smalls[1],
        grad_qkv,
        smalls[2],
        grad_proj,
        smalls[3],
        smalls[4],
        smalls[5],
        smalls[6],
        grad_fc1,
        smalls[7],
        grad_fc2,
        smalls[8],
        smalls[9],
    )


def solution(mesh):
    return jax.shard_map(
        on_device,
        mesh=mesh,
        in_specs=(
            P("gx", "gy"),
            P("gx", "gy"),
            P("gy"),
            P("gy"),
            P("gx", "gy"),
            P("gy"),
            P("gx", "gy"),
            P("gy"),
            P("gy"),
            P("gy"),
            P("gy"),
            P("gx", "gy"),
            P("gy"),
            P("gx", "gy"),
            P("gy"),
            P("gy"),
        ),
        out_specs=(
            P("gx", "gy"),
            P("gx", "gy"),
            P("gy"),
            P("gy"),
            P("gx", "gy"),
            P("gy"),
            P("gx", "gy"),
            P("gy"),
            P("gy"),
            P("gy"),
            P("gy"),
            P("gx", "gy"),
            P("gy"),
            P("gx", "gy"),
            P("gy"),
            P("gy"),
        ),
        check_vma=False,
    )
```
